32 devices in a mesh: dp: 4 (over z), seq: 8 (over y, x, core).
Axes of the slice: x: 2, y: 2, z: 4, core: 2. Of those that a mesh axis runs over, the one named last changes fastest.
Arguments:
- grad_out: bfloat16 [512, 16, 2048], P('seq', 'dp'), may hold values from -12 to 12
- query_in: bfloat16 [512, 16, 2048], P('seq', 'dp'), may hold values from -26 to 26
- rotated_key_input: bfloat16 [512, 16, 512], P('seq', 'dp'), may hold values from -6 to 6
- value_input_columns: bfloat16 [512, 16, 512], P('seq', 'dp'), may hold values from -6 to 6
- out_weight: bfloat16 [2048, 2048], P(None, 'dp'), may hold values from -0.125 to 0.125
- doc_ids: int32 [16, 512], P('dp', 'seq'), may hold values from 0 to 7, never falling along the last dimension, each value on 1 to 128 neighbouring positions
Outputs:
- query_grad: bfloat16 [512, 16, 2048], P('seq', 'dp')
- key_gradient_out: bfloat16 [512, 16, 512], P('seq', 'dp')
- value_gradient_out: bfloat16 [512, 16, 512], P('seq', 'dp')
The draws below stay inside these ranges and needn't reach their ends.
Inputs may be any that keep to these rules, and one draw needn't show every extreme that they name: `doc_ids`: along each sequence the ids never decrease, and every document spans at most 128 positions; in each sequence some document spans exactly 128.
All inputs are finite; a program needn't handle non-finite values.
Results may differ from the reference program's by a relative error of at most 0.04.
Values may be sent and summed in bfloat16 or wider, within the bound.
A program may use at most 128 MiB of HBM per device.

```python
import math
import jax
import jax.numpy as jnp
import numpy as np
from jax import lax

QUERY_HEADS = 16
KEY_VALUE_HEADS = 4
HEAD_SIZE = 128
DOUT = 2048
MAXDOC = 128
SEQUENCE_LENGTH = 512
BATCH_TOTAL = 16


def draw_rotated_key_input(key, part):
    start_offset = jax.random.truncated_normal(jax.random.fold_in(key, 3), -6.0, 6.0, (SEQUENCE_LENGTH, BATCH_TOTAL, KEY_VALUE_HEADS, HEAD_SIZE), jnp.float32)
    return start_offset.reshape(SEQUENCE_LENGTH, BATCH_TOTAL, KEY_VALUE_HEADS * HEAD_SIZE).astype(jnp.bfloat16)


def draw_query_in(key, part):
    start_offset = jax.random.truncated_normal(jax.random.fold_in(key, 5), -6.0, 6.0, (SEQUENCE_LENGTH, BATCH_TOTAL, QUERY_HEADS, HEAD_SIZE), jnp.float32)
    return start_offset.reshape(SEQUENCE_LENGTH, BATCH_TOTAL, QUERY_HEADS * HEAD_SIZE).astype(jnp.bfloat16)


def level_of(own_key, shape, split, low, top_value):
    level, own = 1.0, jax.random.fold_in(own_key, 6)
    for position, blocks in split:
        heights = jnp.exp(jax.random.uniform(jax.random.fold_in(own, position), (blocks,), jnp.float32, low / len(split), top_value / len(split)))
        level = level * jnp.repeat(heights, shape[position] // blocks).reshape([-1 if axis == position else 1 for axis in range(len(shape))])
    return level


def profile(amount, total, most, lean):
    loads = [(1 << 20) // math.isqrt(grade ** lean) + 1 for grade in range(2, amount + 1)]
    spare, counts = total - most - (amount - 1), [1] * (amount - 1)
    while spare > 0:
        free = [i for i in range(amount - 1) if counts[i] < most]
        mass, budget = sum([loads[i] for i in free]), spare
        for i in free:
            addition = min(most - counts[i], max(1, budget * loads[i] // mass), spare)
            counts[i] = counts[i] + addition
            spare = spare - addition
    return np.array([most] + counts)


def ragged_sizes(own_key, number_of, total, reach, lean):
    if number_of == 2:
        one = jax.random.randint(own_key, (), max(1, total - reach), min(reach, total - 1) + 1)
        return jnp.stack([one, total - one])
    lengths = jnp.asarray(profile(number_of, total, reach, lean), jnp.int32)
    pairs = (number_of - 1) // 2
    giver, receiver = lengths[1:1 + 2 * pairs:2], lengths[2:2 + 2 * pairs:2]
    margin = jnp.minimum(giver - 1, reach - receiver)
    passed = jax.random.randint(jax.random.fold_in(own_key, 1), (pairs,), 0, 1 << 20) % (margin + 1)
    lengths = lengths.at[1:1 + 2 * pairs:2].set(giver - passed).at[2:2 + 2 * pairs:2].set(receiver + passed)
    return lengths[jax.random.permutation(jax.random.fold_in(own_key, 2), number_of)]


def noise(stream_key, extent, deviation, bound, shards=(), dtype=jnp.bfloat16):
    result = deviation * jax.random.normal(stream_key, extent, jnp.float32)
    if shards:
        result = result * level_of(stream_key, extent, shards, -0.22, 0.18)
    return jnp.clip(result, -bound, bound).astype(dtype)


def setup_inputs(seed: int = 0) -> dict:
    seeds = jax.random.split(jax.random.key(seed), 7)
    grad_out = noise(seeds[0], (SEQUENCE_LENGTH, BATCH_TOTAL, DOUT), 2.0, 12.0, ((0, 8), (1, 4)))
    query_in = draw_query_in(jax.random.fold_in(seeds[6], 71), 0)
    rotated_key_input = draw_rotated_key_input(jax.random.fold_in(seeds[6], 71), 0)
    value_input_columns = noise(seeds[3], (SEQUENCE_LENGTH, BATCH_TOTAL, KEY_VALUE_HEADS * HEAD_SIZE), 1.0, 6.0, ((0, 8), (1, 4)))
    out_weight = noise(seeds[4], (QUERY_HEADS * HEAD_SIZE, DOUT), DOUT ** -0.5, 0.125, ((1, 4),))
    doc_ids = jax.vmap(lambda own: jnp.searchsorted(jnp.cumsum(ragged_sizes(own, 2 * SEQUENCE_LENGTH // MAXDOC, SEQUENCE_LENGTH, MAXDOC, 0)), jnp.arange(SEQUENCE_LENGTH), side="right"))(jax.random.split(seeds[5], BATCH_TOTAL)).reshape((BATCH_TOTAL, SEQUENCE_LENGTH)).astype(jnp.int32)
    return dict(grad_out=grad_out, query_in=query_in, rotated_key_input=rotated_key_input, value_input_columns=value_input_columns, out_weight=out_weight, doc_ids=doc_ids)


def to_low(full_values):
    return lax.optimization_barrier(full_values.astype(jnp.bfloat16)).astype(jnp.float32)

def sequence_grads(grad_rows, query_rows, key_row_block, value_row_block, doc_row, out_weight):
    heads_per_group = QUERY_HEADS // KEY_VALUE_HEADS
    scale_factor = 1.0 / math.sqrt(HEAD_SIZE)
    d_context = jnp.dot(grad_rows, out_weight.T, preferred_element_type=jnp.float32).astype(jnp.bfloat16)
    query_heads = query_rows.reshape(SEQUENCE_LENGTH, QUERY_HEADS, HEAD_SIZE).astype(jnp.float32)
    grad_heads = d_context.reshape(SEQUENCE_LENGTH, QUERY_HEADS, HEAD_SIZE).astype(jnp.float32)
    key_head_count = jnp.repeat(key_row_block.reshape(SEQUENCE_LENGTH, KEY_VALUE_HEADS, HEAD_SIZE), heads_per_group, axis=1).astype(jnp.float32)
    value_head_count = jnp.repeat(value_row_block.reshape(SEQUENCE_LENGTH, KEY_VALUE_HEADS, HEAD_SIZE), heads_per_group, axis=1).astype(jnp.float32)
    pad_rows = jnp.zeros((MAXDOC, QUERY_HEADS, HEAD_SIZE), jnp.float32)
    key_padded = jnp.concatenate([pad_rows, key_head_count], 0)
    value_padded = jnp.concatenate([pad_rows, value_head_count], 0)
    doc_row = doc_row.astype(jnp.int32)
    doc_padded = jnp.concatenate([jnp.full((MAXDOC,), -1, jnp.int32), doc_row], 0)
    row_block = math.gcd(SEQUENCE_LENGTH, 256)
    window = row_block + MAXDOC
    key_acc = jnp.zeros((SEQUENCE_LENGTH + MAXDOC, QUERY_HEADS, HEAD_SIZE), jnp.float32)
    value_acc = jnp.zeros((SEQUENCE_LENGTH + MAXDOC, QUERY_HEADS, HEAD_SIZE), jnp.float32)
    query_parts = []
    for block_no in range(SEQUENCE_LENGTH // row_block):
        row_start = block_no * row_block
        query_block = query_heads[row_start:row_start + row_block]
        grad_block = grad_heads[row_start:row_start + row_block]
        key_block = key_padded[row_start:row_start + window]
        value_block = value_padded[row_start:row_start + window]
        query_pos = row_start + jnp.arange(row_block)
        key_pos = row_start - MAXDOC + jnp.arange(window)
        allowed = (key_pos[None, :] <= query_pos[:, None]) & (doc_padded[row_start:row_start + window][None, :] == doc_row[row_start:row_start + row_block][:, None])
        scores = jnp.einsum('rhd,whd->hrw', query_block, key_block) * scale_factor
        row_max = lax.optimization_barrier(jnp.max(jnp.where(allowed[None], scores, -jnp.inf), axis=2, keepdims=True))
        raw_weights = jnp.exp(jnp.where(allowed[None], scores - row_max, -jnp.inf))
        weights_soft = raw_weights / lax.optimization_barrier(jnp.sum(raw_weights, axis=2, keepdims=True))
        probs_low = to_low(weights_soft)
        attn_out = to_low(jnp.einsum('hrw,whd->rhd', probs_low, value_block))
        delta_rows = lax.optimization_barrier(jnp.sum(grad_block * attn_out, axis=2))
        value_acc = value_acc.at[row_start:row_start + window].add(jnp.einsum('hrw,rhd->whd', probs_low, grad_block))
        grad_probs = jnp.einsum('rhd,whd->hrw', grad_block, value_block)
        grad_low = to_low(weights_soft * (grad_probs - jnp.transpose(delta_rows)[:, :, None]))
        query_parts.append((jnp.einsum('hrw,whd->rhd', grad_low, key_block) * scale_factor).astype(jnp.bfloat16))
        key_acc = key_acc.at[row_start:row_start + window].add(jnp.einsum('hrw,rhd->whd', grad_low, query_block))
    query_grad = jnp.concatenate(query_parts, 0).reshape(SEQUENCE_LENGTH, QUERY_HEADS * HEAD_SIZE)
    per_head_key_gradient = key_acc[MAXDOC:] * scale_factor
    per_head_value_gradient = value_acc[MAXDOC:]
    key_gradient_out = lax.optimization_barrier(jnp.sum(per_head_key_gradient.reshape(SEQUENCE_LENGTH, KEY_VALUE_HEADS, heads_per_group, HEAD_SIZE), axis=2)).astype(jnp.bfloat16).reshape(SEQUENCE_LENGTH, KEY_VALUE_HEADS * HEAD_SIZE)
    value_gradient_out = lax.optimization_barrier(jnp.sum(per_head_value_gradient.reshape(SEQUENCE_LENGTH, KEY_VALUE_HEADS, heads_per_group, HEAD_SIZE), axis=2)).astype(jnp.bfloat16).reshape(SEQUENCE_LENGTH, KEY_VALUE_HEADS * HEAD_SIZE)
    return (query_grad, key_gradient_out, value_gradient_out)

def reference(grad_out, query_in, rotated_key_input, value_input_columns, out_weight, doc_ids):

    def one_sequence(packed):
        grad_rows, query_rows, key_row_block, value_row_block, doc_row = packed
        return sequence_grads(grad_rows, query_rows, key_row_block, value_row_block, doc_row, out_weight)
    stacked = (jnp.swapaxes(grad_out, 0, 1), jnp.swapaxes(query_in, 0, 1), jnp.swapaxes(rotated_key_input, 0, 1), jnp.swapaxes(value_input_columns, 0, 1), doc_ids)
    query_grad, key_gradient_out, value_gradient_out = lax.map(one_sequence, stacked)
    return (jnp.swapaxes(query_grad, 0, 1), jnp.swapaxes(key_gradient_out, 0, 1), jnp.swapaxes(value_gradient_out, 0, 1))
```

```python
import functools
import math

import jax
import jax.numpy as jnp
from jax import lax
from jax.experimental import pallas as pl
from jax.experimental.pallas import tpu as pltpu
from jax.sharding import PartitionSpec as P

QUERY_HEADS = 16
KEY_VALUE_HEADS = 4
HEAD_SIZE = 128
MAXDOC = 128
GROUP = QUERY_HEADS // KEY_VALUE_HEADS
GROUP_WIDTH = GROUP * HEAD_SIZE
F32 = jnp.float32
BF16 = jnp.bfloat16
NT = (((1,), (1,)), ((), ()))
TN = (((0,), (0,)), ((), ()))


def attention_kernel(
    halo, grad_ref, q_ref, k_ref, v_ref, w_ref, docq_ref, dock_ref,
    dq_ref, dkh_ref, dvh_ref, dko_ref, dvo_ref, bias, probs, dctx
):
    seqs, rows, _ = q_ref.shape
    window = k_ref.shape[1]
    back = halo * rows
    scale = 1.0 / math.sqrt(HEAD_SIZE)
    me = lax.axis_index("seq")

    qpos = lax.broadcasted_iota(jnp.int32, (rows, window), 0) + back
    kpos = lax.broadcasted_iota(jnp.int32, (rows, window), 1)
    causal = (kpos <= qpos) & (kpos + me * rows >= back)
    for b in range(seqs):
        same = dock_ref[b] == docq_ref[b]
        bias[b] = jnp.where(causal & same, 0.0, -1e30).astype(F32)

    def heads(ref, b, start):
        return jnp.concatenate(
            [ref[b, :, pl.ds(pl.multiple_of(start + h * HEAD_SIZE, HEAD_SIZE), HEAD_SIZE)] for h in range(GROUP)], 0
        )

    @pl.loop(0, KEY_VALUE_HEADS)
    def _(g):
        cols = pl.ds(pl.multiple_of(g * HEAD_SIZE, HEAD_SIZE), HEAD_SIZE)

        @pl.loop(0, seqs)
        def _(b):
            s = lax.dot_general(heads(q_ref, b, g * GROUP_WIDTH), k_ref[b, :, cols], NT, preferred_element_type=F32)
            s = s.reshape(GROUP, rows, window) * scale + bias[b][None]
            e = jnp.exp(s - jnp.max(s, axis=2, keepdims=True))
            p = e / jnp.sum(e, axis=2, keepdims=True)
            probs[g * seqs + b] = p.reshape(GROUP * rows, window).astype(BF16)

    @pl.loop(0, KEY_VALUE_HEADS)
    def _(g):
        cols = pl.ds(pl.multiple_of(g * HEAD_SIZE, HEAD_SIZE), HEAD_SIZE)
        wrows = pl.ds(pl.multiple_of(g * GROUP_WIDTH, GROUP_WIDTH), GROUP_WIDTH)
        d = lax.dot_general(grad_ref[...], w_ref[wrows, :], NT, preferred_element_type=F32)
        dctx[...] = d.astype(BF16).reshape(seqs, rows, GROUP_WIDTH)

        @pl.loop(0, seqs)
        def _(b):
            q = heads(q_ref, b, g * GROUP_WIDTH)
            do = heads(dctx, b, 0)
            k = k_ref[b, :, cols]
            p_low = probs[g * seqs + b]
            dp = lax.dot_general(do, v_ref[b, :, cols], NT, preferred_element_type=F32)
            p = p_low.astype(F32)
            delta = jnp.sum(p * dp, axis=1, keepdims=True)
            ds = (p * (dp - delta)).astype(BF16)
            dq = (jnp.dot(ds, k, preferred_element_type=F32) * scale).astype(BF16)
            for h in range(GROUP):
                dst = pl.ds(pl.multiple_of(g * GROUP_WIDTH + h * HEAD_SIZE, HEAD_SIZE), HEAD_SIZE)
                dq_ref[b, :, dst] = dq[h * rows:(h + 1) * rows]
            dk = lax.dot_general(ds, q, TN, preferred_element_type=F32) * scale
            dv = lax.dot_general(p_low, do, TN, preferred_element_type=F32)
            dkh_ref[b, :, cols] = dk[:back].astype(BF16)
            dvh_ref[b, :, cols] = dv[:back].astype(BF16)
            dko_ref[b, :, cols] = dk[back:]
            dvo_ref[b, :, cols] = dv[back:]


def body(grad_out, query_in, rotated_key_input, value_input_columns, out_weight, doc_ids):
    n = lax.axis_size("seq")
    me = lax.axis_index("seq")
    rows, seqs, width = query_in.shape
    halo = -(-(MAXDOC - 1) // rows)
    window = (halo + 1) * rows
    kv_width = rotated_key_input.shape[2]
    rows_each = width // n
    own_rows = lax.dynamic_slice_in_dim(out_weight, me * rows_each, rows_each, 0)
    weight = lax.all_gather(lax.all_gather(own_rows, "dp", axis=1, tiled=True), "seq", axis=0, tiled=True)

    def swap(x):
        return jnp.transpose(x, (1, 0, 2))

    q, grad = swap(query_in), swap(grad_out).reshape(seqs * rows, grad_out.shape[2])
    kv = jnp.stack([swap(rotated_key_input), swap(value_input_columns)])
    docs = doc_ids + 1

    def shift(x, by):
        return lax.ppermute(x, "seq", [(i, (i + by) % n) for i in range(n)])

    steps = range(halo, 0, -1)
    kv_all = jnp.concatenate([shift(kv, s) for s in steps] + [kv], 2)
    docs_all = jnp.concatenate([shift(docs, s) for s in steps] + [docs], 1)
    shapes = (
        jax.ShapeDtypeStruct((seqs, rows, width), BF16),
        jax.ShapeDtypeStruct((seqs, halo * rows, kv_width), BF16),
        jax.ShapeDtypeStruct((seqs, halo * rows, kv_width), BF16),
        jax.ShapeDtypeStruct((seqs, rows, kv_width), F32),
        jax.ShapeDtypeStruct((seqs, rows, kv_width), F32),
    )
    dq, dkh, dvh, dko, dvo = pl.pallas_call(
        functools.partial(attention_kernel, halo),
        out_shape=shapes,
        in_specs=[pl.BlockSpec(memory_space=pltpu.VMEM)] * 7,
        out_specs=[pl.BlockSpec(memory_space=pltpu.VMEM)] * 5,
        scratch_shapes=[
            pltpu.VMEM((seqs, rows, window), F32),
            pltpu.VMEM((KEY_VALUE_HEADS * seqs, GROUP * rows, window), BF16),
            pltpu.VMEM((seqs, rows, GROUP_WIDTH), BF16),
        ],
        compiler_params=pltpu.CompilerParams(vmem_limit_bytes=48 << 20),
    )(grad, q, kv_all[0], kv_all[1], weight, docs[:, :, None], docs_all[:, None, :])
    terms = jnp.stack([dkh, dvh])
    total = jnp.stack([dko, dvo])
    for j, s in enumerate(steps):
        total = total + shift(terms[:, :, j * rows:(j + 1) * rows], -s).astype(F32)
    total = total.astype(BF16)
    return swap(dq), swap(total[0]), swap(total[1])


def solution(mesh):
    in_specs = (
        P("seq", "dp", None),
        P("seq", "dp", None),
        P("seq", "dp", None),
        P("seq", "dp", None),
        P(None, "dp"),
        P("dp", "seq"),
    )
    out_specs = (P("seq", "dp", None), P("seq", "dp", None), P("seq", "dp", None))
    return jax.shard_map(body, mesh=mesh, in_specs=in_specs, out_specs=out_specs, check_vma=False)
```

```python
import functools
import math

import jax
import jax.numpy as jnp
from jax import lax
from jax.experimental import pallas as pl
from jax.experimental.pallas import tpu as pltpu
from jax.sharding import PartitionSpec as P

QUERY_HEADS = 16
KEY_VALUE_HEADS = 4
HEAD_SIZE = 128
MAXDOC = 128
GROUP = QUERY_HEADS // KEY_VALUE_HEADS
GROUP_WIDTH = GROUP * HEAD_SIZE
F32 = jnp.float32
BF16 = jnp.bfloat16
NT = (((1,), (1,)), ((), ()))
TN = (((0,), (0,)), ((), ()))
MESH = pl.DeviceIdType.MESH


def attention_kernel(
    n, depth, halo, chunks,
    grad_ref, q_ref, k_ref, v_ref, w_ref, docq_ref, doc_ref,
    dq_ref, dk_ref, dv_ref,
    bias, probs, dctx, weight, keys, values, docs, parts, landed, own,
    z_send, z_recv, cube_send, cube_recv, halo_send, halo_recv, back_send, back_recv,
):
    seqs, rows, _ = q_ref.shape
    sub, block = w_ref.shape[-2:]
    bits = n.bit_length() - 1
    chunk_width = n * sub
    per_group = chunks // KEY_VALUE_HEADS
    back = halo * rows
    window = back + rows
    scale = 1.0 / math.sqrt(HEAD_SIZE)
    me, layer = lax.axis_index("seq"), lax.axis_index("dp")
    own_bits = [lax.rem(lax.div(me, 1 << b), 2) for b in range(bits)]

    def flip(b):
        return me + (1 - 2 * own_bits[b]) * (1 << b)

    def shifted(by):
        return lax.rem(me + by + n, n)

    barrier = pltpu.get_barrier_semaphore()
    peers = [(lax.rem(layer + j, depth), me) for j in range(1, depth)]
    peers += [(layer, flip(b)) for b in range(bits)]
    peers += [(layer, shifted(s)) for d in range(1, halo + 1) for s in (d, -d)]
    for peer in peers:
        pl.semaphore_signal(barrier, inc=1, device_id=peer, device_id_type=MESH)
    pl.semaphore_wait(barrier, len(peers))

    def remote(src, dst, send, recv, target):
        return pltpu.make_async_remote_copy(
            src_ref=src, dst_ref=dst, send_sem=send, recv_sem=recv, device_id=target, device_id_type=MESH
        )

    mine = tuple(own_bits[b] for b in reversed(range(bits)))
    z_copies = [
        [
            remote(
                w_ref.at[(c,) + mine],
                weight.at[(c,) + mine + (depth - j,)],
                z_send.at[c, j - 1],
                z_recv.at[c, j - 1],
                (lax.rem(layer + j, depth), me),
            )
            for j in range(1, depth)
        ]
        for c in range(chunks)
    ]

    def cube(c, stage):
        high = list(range(1, bits))
        order = (high if c % 2 == 0 else high[::-1]) + [0]
        held = order[:stage]
        where = tuple(slice(None) if b in held else own_bits[b] for b in reversed(range(bits)))
        ref = weight.at[(c,) + where + (pl.ds(1, depth - 1),)]
        return remote(ref, ref, cube_send.at[c, stage], cube_recv.at[c, stage], (layer, flip(order[stage])))

    cube_copies = [[cube(c, s) for s in range(bits)] for c in range(chunks)]

    halo_copies = []
    for d in range(1, halo + 1):
        slot = halo - d
        place = pl.ds(slot * rows, rows)
        for i, (src, dst) in enumerate(
            ((k_ref, keys.at[:, place]), (v_ref, values.at[:, place]), (doc_ref, docs.at[slot]))
        ):
            halo_copies.append(
                remote(src, dst, halo_send.at[slot, i], halo_recv.at[slot, i], (layer, shifted(d)))
            )

    for copy in z_copies[0]:
        copy.start()
    for copy in halo_copies:
        copy.start()
    for c in range(1, chunks):
        for copy in z_copies[c]:
            copy.start()

    keys[:, back:] = k_ref[...]
    values[:, back:] = v_ref[...]
    docs[halo] = doc_ref[...]

    def heads(ref, b, start):
        return jnp.concatenate(
            [ref[b, :, start + h * HEAD_SIZE:start + (h + 1) * HEAD_SIZE] for h in range(GROUP)], 0
        )

    def mask():
        qpos = lax.broadcasted_iota(jnp.int32, (rows, rows), 0) + back
        kpos = lax.broadcasted_iota(jnp.int32, (rows, rows), 1)
        for j in range(halo + 1):
            causal = (kpos + j * rows <= qpos) & (kpos + (j + me) * rows >= back)
            for b in range(seqs):
                same = docs[j, b] == docq_ref[b]
                bias[b, :, j * rows:(j + 1) * rows] = jnp.where(causal & same, 0.0, -1e30).astype(F32)

    def forward(g):
        cols = slice(g * HEAD_SIZE, (g + 1) * HEAD_SIZE)

        @pl.loop(0, seqs)
        def _(b):
            s = lax.dot_general(heads(q_ref, b, g * GROUP_WIDTH), keys[b, :, cols], NT, preferred_element_type=F32)
            s = s.reshape(GROUP, rows, window) * scale + bias[b][None]
            e = jnp.exp(s - jnp.max(s, axis=2, keepdims=True))
            p = e / jnp.sum(e, axis=2, keepdims=True)
            probs[g * seqs + b] = p.reshape(GROUP * rows, window).astype(BF16)

    def project(c):
        d = None
        for j in range(depth):
            at = pl.ds(pl.multiple_of(lax.rem(layer + j, depth) * block, block), block)
            w = w_ref[c] if j == 0 else weight[(c,) + (slice(None),) * bits + (j,)]
            term = lax.dot_general(
                grad_ref[:, at], w.reshape(chunk_width, block), NT, preferred_element_type=F32
            )
            d = term if d is None else d + term
        start = (c % per_group) * chunk_width
        dctx[:, :, start:start + chunk_width] = d.astype(BF16).reshape(seqs, rows, chunk_width)

    def returned(g, j):
        return remote(
            parts.at[g, j], landed.at[g, j], back_send.at[g, j], back_recv.at[g, j], (layer, shifted(j - halo))
        )

    back_copies = [[returned(g, j) for j in range(halo)] for g in range(KEY_VALUE_HEADS)]

    def backward(g):
        cols = slice(g * HEAD_SIZE, (g + 1) * HEAD_SIZE)

        @pl.loop(0, seqs)
        def _(b):
            q = heads(q_ref, b, g * GROUP_WIDTH)
            do = heads(dctx, b, 0)
            k = keys[b, :, cols]
            p_low = probs[g * seqs + b]
            dp = lax.dot_general(do, values[b, :, cols], NT, preferred_element_type=F32)
            p = p_low.astype(F32)
            delta = jnp.sum(p * dp, axis=1, keepdims=True)
            ds = (p * (dp - delta)).astype(BF16)
            dq = (jnp.dot(ds, k, preferred_element_type=F32) * scale).astype(BF16)
            for h in range(GROUP):
                start = g * GROUP_WIDTH + h * HEAD_SIZE
                dq_ref[b, :, start:start + HEAD_SIZE] = dq[h * rows:(h + 1) * rows]
            dk = lax.dot_general(ds, q, TN, preferred_element_type=F32) * scale
            dv = lax.dot_general(p_low, do, TN, preferred_element_type=F32)
            for i, term in enumerate((dk, dv)):
                for j in range(halo):
                    parts[g, j, i, b] = term[j * rows:(j + 1) * rows].astype(BF16)
                own[g, i, b] = term[back:]

        for copy in back_copies[g]:
            copy.start()

    def finish(g):
        cols = slice(g * HEAD_SIZE, (g + 1) * HEAD_SIZE)
        for copy in back_copies[g]:
            copy.wait_recv()
        for i, out in enumerate((dk_ref, dv_ref)):
            total = own[g, i]
            for j in range(halo):
                total = total + landed[g, j, i].astype(F32)
            out[:, :, cols] = total.astype(BF16)

    for step in range(chunks + bits):
        for stage in range(bits, -1, -1):
            c = step - stage
            if not 0 <= c < chunks:
                continue
            if stage == 0:
                for copy in z_copies[c]:
                    copy.wait_recv()
            else:
                cube_copies[c][stage - 1].wait_recv()
            if stage < bits:
                cube_copies[c][stage].start()
        if step == 0:
            for copy in halo_copies:
                copy.wait_recv()
            mask()
        if step < KEY_VALUE_HEADS:
            forward(step)
        c = step - bits
        if c >= 0:
            project(c)
            if c % per_group == per_group - 1:
                backward(c // per_group)
                if c // per_group > 0:
                    finish(c // per_group - 1)
    finish(KEY_VALUE_HEADS - 1)

    for copy in halo_copies + sum(z_copies, []) + sum(cube_copies, []) + sum(back_copies, []):
        copy.wait_send()


def body(grad_out, query_in, rotated_key_input, value_input_columns, out_weight, doc_ids):
    n, depth = lax.axis_size("seq"), lax.axis_size("dp")
    rows, seqs, width = query_in.shape
    features, block = out_weight.shape
    bits = n.bit_length() - 1
    halo = -(-(MAXDOC - 1) // rows)
    window = (halo + 1) * rows
    kv_width = rotated_key_input.shape[2]
    chunks = KEY_VALUE_HEADS * max(1, min(2, features // (KEY_VALUE_HEADS * n * 16)))
    sub = features // (chunks * n)
    cube = (chunks,) + (2,) * bits

    def swap(x):
        return jnp.transpose(x, (1, 0, 2))

    q, grad = swap(query_in), swap(grad_out).reshape(seqs * rows, grad_out.shape[2])
    shapes = (
        jax.ShapeDtypeStruct((seqs, rows, width), BF16),
        jax.ShapeDtypeStruct((seqs, rows, kv_width), BF16),
        jax.ShapeDtypeStruct((seqs, rows, kv_width), BF16),
    )
    dma = pltpu.SemaphoreType.DMA
    dq, dk, dv = pl.pallas_call(
        functools.partial(attention_kernel, n, depth, halo, chunks),
        out_shape=shapes,
        in_specs=[pl.BlockSpec(memory_space=pltpu.VMEM)] * 7,
        out_specs=[pl.BlockSpec(memory_space=pltpu.VMEM)] * 3,
        scratch_shapes=[
            pltpu.VMEM((seqs, rows, window), F32),
            pltpu.VMEM((KEY_VALUE_HEADS * seqs, GROUP * rows, window), BF16),
            pltpu.VMEM((seqs, rows, GROUP_WIDTH), BF16),
            pltpu.VMEM(cube + (depth, sub, block), BF16),
            pltpu.VMEM((seqs, window, kv_width), BF16),
            pltpu.VMEM((seqs, window, kv_width), BF16),
            pltpu.VMEM((halo + 1, seqs, 1, rows), jnp.int32),
            pltpu.VMEM((KEY_VALUE_HEADS, halo, 2, seqs, rows, HEAD_SIZE), BF16),
            pltpu.VMEM((KEY_VALUE_HEADS, halo, 2, seqs, rows, HEAD_SIZE), BF16),
            pltpu.VMEM((KEY_VALUE_HEADS, 2, seqs, rows, HEAD_SIZE), F32),
            dma((chunks, depth - 1)),
            dma((chunks, depth - 1)),
            dma((chunks, bits)),
            dma((chunks, bits)),
            dma((halo, 3)),
            dma((halo, 3)),
            dma((KEY_VALUE_HEADS, halo)),
            dma((KEY_VALUE_HEADS, halo)),
        ],
        compiler_params=pltpu.CompilerParams(
            vmem_limit_bytes=48 << 20, collective_id=0, has_side_effects=True
        ),
    )(
        grad, q, swap(rotated_key_input), swap(value_input_columns),
        out_weight.reshape(cube + (sub, block)), doc_ids[:, :, None], doc_ids[:, None, :],
    )
    return swap(dq), swap(dk), swap(dv)


def solution(mesh):
    in_specs = (
        P("seq", "dp", None),
        P("seq", "dp", None),
        P("seq", "dp", None),
        P("seq", "dp", None),
        P(None, "dp"),
        P("dp", "seq"),
    )
    out_specs = (P("seq", "dp", None), P("seq", "dp", None), P("seq", "dp", None))
    return jax.shard_map(body, mesh=mesh, in_specs=in_specs, out_specs=out_specs, check_vma=False)
```

```python
import functools
import math

import jax
import jax.numpy as jnp
from jax import lax
from jax.experimental import pallas as pl
from jax.experimental.pallas import tpu as pltpu
from jax.sharding import PartitionSpec as P

QUERY_HEADS = 16
KEY_VALUE_HEADS = 4
HEAD_SIZE = 128
MAXDOC = 128
GROUP = QUERY_HEADS // KEY_VALUE_HEADS
GROUP_WIDTH = GROUP * HEAD_SIZE
F32 = jnp.float32
BF16 = jnp.bfloat16
NT = (((1,), (1,)), ((), ()))
TN = (((0,), (0,)), ((), ()))
MESH = pl.DeviceIdType.MESH


def attention_kernel(
    n, depth, halo, chunks,
    grad_ref, q_ref, k_ref, v_ref, w_ref, docq_ref, doc_ref,
    dq_ref, dk_ref, dv_ref,
    bias, probs, dctx, weight, keys, values, docs, parts, landed, own,
    z_send, z_recv, cube_send, cube_recv, halo_send, halo_recv, back_send, back_recv,
):
    seqs, rows, _ = q_ref.shape
    sub, block = w_ref.shape[-2:]
    bits = n.bit_length() - 1
    chunk_width = n * sub
    per_group = chunks // KEY_VALUE_HEADS
    back = halo * rows
    window = back + rows
    scale = 1.0 / math.sqrt(HEAD_SIZE)
    me, layer = lax.axis_index("seq"), lax.axis_index("dp")
    own_bits = [lax.rem(lax.div(me, 1 << b), 2) for b in range(bits)]

    def flip(b):
        return me + (1 - 2 * own_bits[b]) * (1 << b)

    def shifted(by):
        return lax.rem(me + by + n, n)

    barrier = pltpu.get_barrier_semaphore()
    peers = [(lax.rem(layer + j, depth), me) for j in range(1, depth)]
    peers += [(layer, flip(b)) for b in range(bits)]
    peers += [(layer, shifted(s)) for s in (1, -1)]
    for peer in peers:
        pl.semaphore_signal(barrier, inc=1, device_id=peer, device_id_type=MESH)
    pl.semaphore_wait(barrier, len(peers))

    def remote(src, dst, send, recv, target):
        return pltpu.make_async_remote_copy(
            src_ref=src, dst_ref=dst, send_sem=send, recv_sem=recv, device_id=target, device_id_type=MESH
        )

    mine = tuple(own_bits[b] for b in reversed(range(bits)))
    z_copies = [
        [
            remote(
                w_ref.at[(c,) + mine],
                weight.at[(c,) + mine + (depth - j,)],
                z_send.at[c, j - 1],
                z_recv.at[c, j - 1],
                (lax.rem(layer + j, depth), me),
            )
            for j in range(1, depth)
        ]
        for c in range(chunks)
    ]

    def cube(c, stage):
        high = list(range(1, bits))
        order = high + [0]
        held = order[:stage]
        where = tuple(slice(None) if b in held else own_bits[b] for b in reversed(range(bits)))
        ref = weight.at[(c,) + where + (pl.ds(1, depth - 1),)]
        return remote(ref, ref, cube_send.at[c, stage], cube_recv.at[c, stage], (layer, flip(order[stage])))

    cube_copies = [[cube(c, s) for s in range(bits)] for c in range(chunks)]

    halo_copies = []
    for hop in range(halo):
        slot = halo - 1 - hop
        place, source = pl.ds(slot * rows, rows), pl.ds((slot + 1) * rows, rows)
        pairs = (
            (k_ref if hop == 0 else keys.at[:, source], keys.at[:, place]),
            (v_ref if hop == 0 else values.at[:, source], values.at[:, place]),
            (doc_ref if hop == 0 else docs.at[slot + 1], docs.at[slot]),
        )
        halo_copies.append(
            [
                remote(src, dst, halo_send.at[hop, i], halo_recv.at[hop, i], (layer, shifted(1)))
                for i, (src, dst) in enumerate(pairs)
            ]
        )

    for copy in z_copies[0]:
        copy.start()
    for copy in halo_copies[0]:
        copy.start()
    for c in range(1, chunks):
        for copy in z_copies[c]:
            copy.start()

    keys[:, back:] = k_ref[...]
    values[:, back:] = v_ref[...]
    docs[halo] = doc_ref[...]

    def heads(ref, b, start):
        return jnp.concatenate(
            [ref[b, :, start + h * HEAD_SIZE:start + (h + 1) * HEAD_SIZE] for h in range(GROUP)], 0
        )

    def mask():
        qpos = lax.broadcasted_iota(jnp.int32, (rows, rows), 0) + back
        kpos = lax.broadcasted_iota(jnp.int32, (rows, rows), 1)
        for j in range(halo + 1):
            causal = (kpos + j * rows <= qpos) & (kpos + (j + me) * rows >= back)
            for b in range(seqs):
                same = docs[j, b] == docq_ref[b]
                bias[b, :, j * rows:(j + 1) * rows] = jnp.where(causal & same, 0.0, -1e30).astype(F32)

    def forward(g):
        cols = slice(g * HEAD_SIZE, (g + 1) * HEAD_SIZE)

        @pl.loop(0, seqs)
        def _(b):
            s = lax.dot_general(heads(q_ref, b, g * GROUP_WIDTH), keys[b, :, cols], NT, preferred_element_type=F32)
            s = s.reshape(GROUP, rows, window) * scale + bias[b][None]
            e = jnp.exp(s - jnp.max(s, axis=2, keepdims=True))
            p = e / jnp.sum(e, axis=2, keepdims=True)
            probs[g * seqs + b] = p.reshape(GROUP * rows, window).astype(BF16)

    def project(c):
        d = None
        for j in range(depth):
            at = pl.ds(pl.multiple_of(lax.rem(layer + j, depth) * block, block), block)
            w = w_ref[c] if j == 0 else weight[(c,) + (slice(None),) * bits + (j,)]
            term = lax.dot_general(
                grad_ref[:, at], w.reshape(chunk_width, block), NT, preferred_element_type=F32
            )
            d = term if d is None else d + term
        start = (c % per_group) * chunk_width
        dctx[:, :, start:start + chunk_width] = d.astype(BF16).reshape(seqs, rows, chunk_width)

    def returned(g, j):
        return remote(
            parts.at[g, j], landed.at[g, j], back_send.at[g, j], back_recv.at[g, j], (layer, shifted(-1))
        )

    back_copies = [[returned(g, j) for j in range(halo)] for g in range(KEY_VALUE_HEADS)]

    def backward(g):
        cols = slice(g * HEAD_SIZE, (g + 1) * HEAD_SIZE)

        @pl.loop(0, seqs)
        def _(b):
            q = heads(q_ref, b, g * GROUP_WIDTH)
            do = heads(dctx, b, 0)
            k = keys[b, :, cols]
            p_low = probs[g * seqs + b]
            dp = lax.dot_general(do, values[b, :, cols], NT, preferred_element_type=F32)
            p = p_low.astype(F32)
            delta = jnp.sum(p * dp, axis=1, keepdims=True)
            ds = (p * (dp - delta)).astype(BF16)
            dq = (jnp.dot(ds, k, preferred_element_type=F32) * scale).astype(BF16)
            for h in range(GROUP):
                start = g * GROUP_WIDTH + h * HEAD_SIZE
                dq_ref[b, :, start:start + HEAD_SIZE] = dq[h * rows:(h + 1) * rows]
            dk = lax.dot_general(ds, q, TN, preferred_element_type=F32) * scale
            dv = lax.dot_general(p_low, do, TN, preferred_element_type=F32)
            for i, term in enumerate((dk, dv)):
                for j in range(halo):
                    parts[g, j, i, b] = term[j * rows:(j + 1) * rows].astype(BF16)
                own[g, i, b] = term[back:]

        back_copies[g][0].start()

    def relay(g):
        for j in range(1, halo):
            back_copies[g][j - 1].wait_recv()
            parts[g, j] = (parts[g, j].astype(F32) + landed[g, j - 1].astype(F32)).astype(BF16)
            back_copies[g][j].start()

    def finish(g):
        cols = slice(g * HEAD_SIZE, (g + 1) * HEAD_SIZE)
        back_copies[g][halo - 1].wait_recv()
        for i, out in enumerate((dk_ref, dv_ref)):
            out[:, :, cols] = (own[g, i] + landed[g, halo - 1, i].astype(F32)).astype(BF16)

    for step in range(chunks + bits):
        for stage in range(bits, -1, -1):
            c = step - stage
            if not 0 <= c < chunks:
                continue
            if stage == 0:
                for copy in z_copies[c]:
                    copy.wait_recv()
            else:
                cube_copies[c][stage - 1].wait_recv()
            if stage < bits:
                cube_copies[c][stage].start()
        if step < halo:
            for copy in halo_copies[step]:
                copy.wait_recv()
            if step + 1 < halo:
                for copy in halo_copies[step + 1]:
                    copy.start()
            else:
                mask()
        if 0 <= step - halo + 1 < KEY_VALUE_HEADS:
            forward(step - halo + 1)
        c = step - bits
        if c >= 0:
            project(c)
            if c % per_group == per_group - 1:
                group = c // per_group
                if group > 0:
                    relay(group - 1)
                backward(group)
                if group > 0:
                    finish(group - 1)
    relay(KEY_VALUE_HEADS - 1)
    finish(KEY_VALUE_HEADS - 1)

    for copy in sum(halo_copies, []) + sum(z_copies, []) + sum(cube_copies, []) + sum(back_copies, []):
        copy.wait_send()


def body(grad_out, query_in, rotated_key_input, value_input_columns, out_weight, doc_ids):
    n, depth = lax.axis_size("seq"), lax.axis_size("dp")
    rows, seqs, width = query_in.shape
    features, block = out_weight.shape
    bits = n.bit_length() - 1
    halo = -(-(MAXDOC - 1) // rows)
    window = (halo + 1) * rows
    kv_width = rotated_key_input.shape[2]
    chunks = KEY_VALUE_HEADS * max(1, min(2, features // (KEY_VALUE_HEADS * n * 16)))
    sub = features // (chunks * n)
    cube = (chunks,) + (2,) * bits

    def swap(x):
        return jnp.transpose(x, (1, 0, 2))

    q, grad = swap(query_in), swap(grad_out).reshape(seqs * rows, grad_out.shape[2])
    shapes = (
        jax.ShapeDtypeStruct((seqs, rows, width), BF16),
        jax.ShapeDtypeStruct((seqs, rows, kv_width), BF16),
        jax.ShapeDtypeStruct((seqs, rows, kv_width), BF16),
    )
    dma = pltpu.SemaphoreType.DMA
    dq, dk, dv = pl.pallas_call(
        functools.partial(attention_kernel, n, depth, halo, chunks),
        out_shape=shapes,
        in_specs=[pl.BlockSpec(memory_space=pltpu.VMEM)] * 7,
        out_specs=[pl.BlockSpec(memory_space=pltpu.VMEM)] * 3,
        scratch_shapes=[
            pltpu.VMEM((seqs, rows, window), F32),
            pltpu.VMEM((KEY_VALUE_HEADS * seqs, GROUP * rows, window), BF16),
            pltpu.VMEM((seqs, rows, GROUP_WIDTH), BF16),
            pltpu.VMEM(cube + (depth, sub, block), BF16),
            pltpu.VMEM((seqs, window, kv_width), BF16),
            pltpu.VMEM((seqs, window, kv_width), BF16),
            pltpu.VMEM((halo + 1, seqs, 1, rows), jnp.int32),
            pltpu.VMEM((KEY_VALUE_HEADS, halo, 2, seqs, rows, HEAD_SIZE), BF16),
            pltpu.VMEM((KEY_VALUE_HEADS, halo, 2, seqs, rows, HEAD_SIZE), BF16),
            pltpu.VMEM((KEY_VALUE_HEADS, 2, seqs, rows, HEAD_SIZE), F32),
            dma((chunks, depth - 1)),
            dma((chunks, depth - 1)),
            dma((chunks, bits)),
            dma((chunks, bits)),
            dma((halo, 3)),
            dma((halo, 3)),
            dma((KEY_VALUE_HEADS, halo)),
            dma((KEY_VALUE_HEADS, halo)),
        ],
        compiler_params=pltpu.CompilerParams(
            vmem_limit_bytes=48 << 20, collective_id=0, has_side_effects=True
        ),
    )(
        grad, q, swap(rotated_key_input), swap(value_input_columns),
        out_weight.reshape(cube + (sub, block)), doc_ids[:, :, None], doc_ids[:, None, :],
    )
    return swap(dq), swap(dk), swap(dv)


def solution(mesh):
    in_specs = (
        P("seq", "dp", None),
        P("seq", "dp", None),
        P("seq", "dp", None),
        P("seq", "dp", None),
        P(None, "dp"),
        P("dp", "seq"),
    )
    out_specs = (P("seq", "dp", None), P("seq", "dp", None), P("seq", "dp", None))
    return jax.shard_map(body, mesh=mesh, in_specs=in_specs, out_specs=out_specs, check_vma=False)
```

```python
import functools
import math

import jax
import jax.numpy as jnp
from jax import lax
from jax.experimental import pallas as pl
from jax.experimental.pallas import tpu as pltpu
from jax.sharding import PartitionSpec as P

QUERY_HEADS = 16
KEY_VALUE_HEADS = 4
HEAD_SIZE = 128
MAXDOC = 128
GROUP = QUERY_HEADS // KEY_VALUE_HEADS
GROUP_WIDTH = GROUP * HEAD_SIZE
F32 = jnp.float32
BF16 = jnp.bfloat16
NT = (((1,), (1,)), ((), ()))
TN = (((0,), (0,)), ((), ()))
MESH = pl.DeviceIdType.MESH
LAG = 2


def attention_kernel(
    n, depth, halo, chunks,
    grad_ref, q_ref, k_ref, v_ref, w_ref, docq_ref, doc_ref,
    dq_ref, dk_ref, dv_ref,
    bias, probs, dctx, weight, keys, values, docs, parts, landed, own,
    z_send, z_recv, cube_send, cube_recv, halo_send, halo_recv, back_send, back_recv,
):
    seqs, rows, _ = q_ref.shape
    sub, block = w_ref.shape[-2:]
    bits = n.bit_length() - 1
    per_group = chunks // KEY_VALUE_HEADS
    back = halo * rows
    window = back + rows
    scale = 1.0 / math.sqrt(HEAD_SIZE)
    me, layer = lax.axis_index("seq"), lax.axis_index("dp")
    own_bits = [lax.rem(lax.div(me, 1 << b), 2) for b in range(bits)]

    def flip(b):
        return me + (1 - 2 * own_bits[b]) * (1 << b)

    def shifted(by):
        return lax.rem(me + by + n, n)

    barrier = pltpu.get_barrier_semaphore()
    peers = [(lax.rem(layer + j, depth), me) for j in range(1, depth)]
    peers += [(layer, flip(b)) for b in range(bits)]
    peers += [(layer, shifted(s)) for s in (1, -1)]
    for peer in peers:
        pl.semaphore_signal(barrier, inc=1, device_id=peer, device_id_type=MESH)
    pl.semaphore_wait(barrier, len(peers))

    def remote(src, dst, send, recv, target):
        return pltpu.make_async_remote_copy(
            src_ref=src, dst_ref=dst, send_sem=send, recv_sem=recv, device_id=target, device_id_type=MESH
        )

    mine = tuple(own_bits[b] for b in reversed(range(bits)))
    z_copies = [
        [
            remote(
                w_ref.at[(c,) + mine],
                weight.at[(c,) + mine + (depth - j,)],
                z_send.at[c, j - 1],
                z_recv.at[c, j - 1],
                (lax.rem(layer + j, depth), me),
            )
            for j in range(1, depth)
        ]
        for c in range(chunks)
    ]

    def cube(c, stage):
        high = list(range(1, bits))
        order = (high if c % 2 == 0 else high[::-1]) + [0]
        held = order[:stage]
        where = tuple(slice(None) if b in held else own_bits[b] for b in reversed(range(bits)))
        ref = weight.at[(c,) + where + (pl.ds(1, depth - 1),)]
        return remote(ref, ref, cube_send.at[c, stage], cube_recv.at[c, stage], (layer, flip(order[stage])))

    cube_copies = [[cube(c, s) for s in range(bits)] for c in range(chunks)]

    halo_copies = []
    for hop in range(halo):
        slot = halo - 1 - hop
        place, source = pl.ds(slot * rows, rows), pl.ds((slot + 1) * rows, rows)
        pairs = (
            (k_ref if hop == 0 else keys.at[:, source], keys.at[:, place]),
            (v_ref if hop == 0 else values.at[:, source], values.at[:, place]),
            (doc_ref if hop == 0 else docs.at[slot + 1], docs.at[slot]),
        )
        halo_copies.append(
            [
                remote(src, dst, halo_send.at[hop, i], halo_recv.at[hop, i], (layer, shifted(1)))
                for i, (src, dst) in enumerate(pairs)
            ]
        )

    for copy in z_copies[0]:
        copy.start()
    for copy in halo_copies[0]:
        copy.start()
    for c in range(1, chunks):
        for copy in z_copies[c]:
            copy.start()

    keys[:, back:] = k_ref[...]
    values[:, back:] = v_ref[...]
    docs[halo] = doc_ref[...]

    def heads(ref, b, start):
        return jnp.concatenate(
            [ref[b, :, start + h * HEAD_SIZE:start + (h + 1) * HEAD_SIZE] for h in range(GROUP)], 0
        )

    def mask():
        qpos = lax.broadcasted_iota(jnp.int32, (rows, rows), 0) + back
        kpos = lax.broadcasted_iota(jnp.int32, (rows, rows), 1)
        for j in range(halo + 1):
            causal = (kpos + j * rows <= qpos) & (kpos + (j + me) * rows >= back)
            for b in range(seqs):
                same = docs[j, b] == docq_ref[b]
                bias[b, :, j * rows:(j + 1) * rows] = jnp.where(causal & same, 0.0, -1e30).astype(F32)

    def forward(g):
        cols = slice(g * HEAD_SIZE, (g + 1) * HEAD_SIZE)

        @pl.loop(0, seqs)
        def _(b):
            s = lax.dot_general(heads(q_ref, b, g * GROUP_WIDTH), keys[b, :, cols], NT, preferred_element_type=F32)
            s = s.reshape(GROUP, rows, window) * scale + bias[b][None]
            e = jnp.exp(s - jnp.max(s, axis=2, keepdims=True))
            p = e / jnp.sum(e, axis=2, keepdims=True)
            probs[g * seqs + b] = p.reshape(GROUP * rows, window).astype(BF16)

    def project(g):
        d = None
        span = slice(g * per_group, (g + 1) * per_group)
        for j in range(depth):
            at = pl.ds(pl.multiple_of(lax.rem(layer + j, depth) * block, block), block)
            w = w_ref[span] if j == 0 else weight[(span,) + (slice(None),) * bits + (j,)]
            term = lax.dot_general(
                grad_ref[:, at], w.reshape(GROUP_WIDTH, block), NT, preferred_element_type=F32
            )
            d = term if d is None else d + term
        dctx[...] = d.astype(BF16).reshape(seqs, rows, GROUP_WIDTH)

    def returned(g, j):
        return remote(
            parts.at[g, j], landed.at[g, j], back_send.at[g, j], back_recv.at[g, j], (layer, shifted(-1))
        )

    back_copies = [[returned(g, j) for j in range(halo)] for g in range(KEY_VALUE_HEADS)]

    def backward(g):
        cols = slice(g * HEAD_SIZE, (g + 1) * HEAD_SIZE)

        @pl.loop(0, seqs)
        def _(b):
            q = heads(q_ref, b, g * GROUP_WIDTH)
            do = heads(dctx, b, 0)
            k = keys[b, :, cols]
            p_low = probs[g * seqs + b]
            dp = lax.dot_general(do, values[b, :, cols], NT, preferred_element_type=F32)
            p = p_low.astype(F32)
            delta = jnp.sum(p * dp, axis=1, keepdims=True)
            ds = (p * (dp - delta)).astype(BF16)
            dq = (jnp.dot(ds, k, preferred_element_type=F32) * scale).astype(BF16)
            for h in range(GROUP):
                start = g * GROUP_WIDTH + h * HEAD_SIZE
                dq_ref[b, :, start:start + HEAD_SIZE] = dq[h * rows:(h + 1) * rows]
            dk = lax.dot_general(ds, q, TN, preferred_element_type=F32) * scale
            dv = lax.dot_general(p_low, do, TN, preferred_element_type=F32)
            for i, term in enumerate((dk, dv)):
                for j in range(halo):
                    parts[g, j, i, b] = term[j * rows:(j + 1) * rows].astype(BF16)
                own[g, i, b] = term[back:]

        back_copies[g][0].start()

    def relay(g):
        for j in range(1, halo):
            back_copies[g][j - 1].wait_recv()
            parts[g, j] = (parts[g, j].astype(F32) + landed[g, j - 1].astype(F32)).astype(BF16)
            back_copies[g][j].start()

    def finish(g):
        cols = slice(g * HEAD_SIZE, (g + 1) * HEAD_SIZE)
        back_copies[g][halo - 1].wait_recv()
        for i, out in enumerate((dk_ref, dv_ref)):
            out[:, :, cols] = (own[g, i] + landed[g, halo - 1, i].astype(F32)).astype(BF16)

    for step in range(chunks + LAG * bits):
        for stage in range(bits, -1, -1):
            c = step - LAG * stage
            if not 0 <= c < chunks:
                continue
            if stage == 0:
                for copy in z_copies[c]:
                    copy.wait_recv()
            else:
                cube_copies[c][stage - 1].wait_recv()
            if stage < bits:
                cube_copies[c][stage].start()
        if step < halo:
            for copy in halo_copies[step]:
                copy.wait_recv()
            if step + 1 < halo:
                for copy in halo_copies[step + 1]:
                    copy.start()
            else:
                mask()
        if 0 <= step - halo + 1 < KEY_VALUE_HEADS:
            forward(step - halo + 1)
        c = step - LAG * bits
        if c >= 0 and c % per_group == per_group - 1:
            group = c // per_group
            project(group)
            if group > 0:
                relay(group - 1)
            backward(group)
            if group > 0:
                finish(group - 1)
    relay(KEY_VALUE_HEADS - 1)
    finish(KEY_VALUE_HEADS - 1)

    for copy in sum(halo_copies, []) + sum(z_copies, []) + sum(cube_copies, []) + sum(back_copies, []):
        copy.wait_send()


def body(grad_out, query_in, rotated_key_input, value_input_columns, out_weight, doc_ids):
    n, depth = lax.axis_size("seq"), lax.axis_size("dp")
    rows, seqs, width = query_in.shape
    features, block = out_weight.shape
    bits = n.bit_length() - 1
    halo = -(-(MAXDOC - 1) // rows)
    window = (halo + 1) * rows
    kv_width = rotated_key_input.shape[2]
    chunks = KEY_VALUE_HEADS * max(1, min(2, features // (KEY_VALUE_HEADS * n * 16)))
    sub = features // (chunks * n)
    cube = (chunks,) + (2,) * bits

    def swap(x):
        return jnp.transpose(x, (1, 0, 2))

    q, grad = swap(query_in), swap(grad_out).reshape(seqs * rows, grad_out.shape[2])
    shapes = (
        jax.ShapeDtypeStruct((seqs, rows, width), BF16),
        jax.ShapeDtypeStruct((seqs, rows, kv_width), BF16),
        jax.ShapeDtypeStruct((seqs, rows, kv_width), BF16),
    )
    dma = pltpu.SemaphoreType.DMA
    dq, dk, dv = pl.pallas_call(
        functools.partial(attention_kernel, n, depth, halo, chunks),
        out_shape=shapes,
        in_specs=[pl.BlockSpec(memory_space=pltpu.VMEM)] * 7,
        out_specs=[pl.BlockSpec(memory_space=pltpu.VMEM)] * 3,
        scratch_shapes=[
            pltpu.VMEM((seqs, rows, window), F32),
            pltpu.VMEM((KEY_VALUE_HEADS * seqs, GROUP * rows, window), BF16),
            pltpu.VMEM((seqs, rows, GROUP_WIDTH), BF16),
            pltpu.VMEM(cube + (depth, sub, block), BF16),
            pltpu.VMEM((seqs, window, kv_width), BF16),
            pltpu.VMEM((seqs, window, kv_width), BF16),
            pltpu.VMEM((halo + 1, seqs, 1, rows), jnp.int32),
            pltpu.VMEM((KEY_VALUE_HEADS, halo, 2, seqs, rows, HEAD_SIZE), BF16),
            pltpu.VMEM((KEY_VALUE_HEADS, halo, 2, seqs, rows, HEAD_SIZE), BF16),
            pltpu.VMEM((KEY_VALUE_HEADS, 2, seqs, rows, HEAD_SIZE), F32),
            dma((chunks, depth - 1)),
            dma((chunks, depth - 1)),
            dma((chunks, bits)),
            dma((chunks, bits)),
            dma((halo, 3)),
            dma((halo, 3)),
            dma((KEY_VALUE_HEADS, halo)),
            dma((KEY_VALUE_HEADS, halo)),
        ],
        compiler_params=pltpu.CompilerParams(
            vmem_limit_bytes=48 << 20, collective_id=0, has_side_effects=True
        ),
    )(
        grad, q, swap(rotated_key_input), swap(value_input_columns),
        out_weight.reshape(cube + (sub, block)), doc_ids[:, :, None], doc_ids[:, None, :],
    )
    return swap(dq), swap(dk), swap(dv)


def solution(mesh):
    in_specs = (
        P("seq", "dp", None),
        P("seq", "dp", None),
        P("seq", "dp", None),
        P("seq", "dp", None),
        P(None, "dp"),
        P("dp", "seq"),
    )
    out_specs = (P("seq", "dp", None), P("seq", "dp", None), P("seq", "dp", None))
    return jax.shard_map(body, mesh=mesh, in_specs=in_specs, out_specs=out_specs, check_vma=False)
```

```python
import functools
import math

import jax
import jax.numpy as jnp
from jax import lax
from jax.experimental import pallas as pl
from jax.experimental.pallas import tpu as pltpu
from jax.sharding import PartitionSpec as P

QUERY_HEADS = 16
KEY_VALUE_HEADS = 4
HEAD_SIZE = 128
MAXDOC = 128
GROUP = QUERY_HEADS // KEY_VALUE_HEADS
GROUP_WIDTH = GROUP * HEAD_SIZE
F32 = jnp.float32
BF16 = jnp.bfloat16
NT = (((1,), (1,)), ((), ()))
TN = (((0,), (0,)), ((), ()))
MESH = pl.DeviceIdType.MESH
LAG = 2


def attention_kernel(
    n, depth, halo, chunks,
    grad_ref, q_ref, k_ref, v_ref, w_ref, docq_ref, doc_ref,
    dq_ref, dk_ref, dv_ref,
    bias, probs, dctx, weight, keys, values, docs, parts, landed, own,
    z_send, z_recv, cube_send, cube_recv, halo_send, halo_recv, back_send, back_recv,
):
    seqs, rows, _ = q_ref.shape
    sub, block = w_ref.shape[-2:]
    bits = n.bit_length() - 1
    per_group = chunks // KEY_VALUE_HEADS
    back = halo * rows
    window = back + rows
    scale = 1.0 / math.sqrt(HEAD_SIZE)
    me, layer = lax.axis_index("seq"), lax.axis_index("dp")
    own_bits = [lax.rem(lax.div(me, 1 << b), 2) for b in range(bits)]

    def flip(b):
        return me + (1 - 2 * own_bits[b]) * (1 << b)

    def shifted(by):
        return lax.rem(me + by + n, n)

    barrier = pltpu.get_barrier_semaphore()
    peers = [(lax.rem(layer + j, depth), me) for j in range(1, depth)]
    peers += [(layer, flip(b)) for b in range(bits)]
    peers += [(layer, shifted(s)) for s in (1, -1)]
    for peer in peers:
        pl.semaphore_signal(barrier, inc=1, device_id=peer, device_id_type=MESH)
    pl.semaphore_wait(barrier, len(peers))

    def remote(src, dst, send, recv, target):
        return pltpu.make_async_remote_copy(
            src_ref=src, dst_ref=dst, send_sem=send, recv_sem=recv, device_id=target, device_id_type=MESH
        )

    mine = tuple(own_bits[b] for b in reversed(range(bits)))
    z_copies = [
        [
            remote(
                w_ref.at[(c,) + mine],
                weight.at[(c,) + mine + (depth - j,)],
                z_send.at[c, j - 1],
                z_recv.at[c, j - 1],
                (lax.rem(layer + j, depth), me),
            )
            for j in range(1, depth)
        ]
        for c in range(chunks)
    ]

    def cube(c, stage):
        high = list(range(1, bits))
        order = (high if c % 2 == 0 else high[::-1]) + [0]
        held = order[:stage]
        where = tuple(slice(None) if b in held else own_bits[b] for b in reversed(range(bits)))
        ref = weight.at[(c,) + where + (pl.ds(1, depth - 1),)]
        return remote(ref, ref, cube_send.at[c, stage], cube_recv.at[c, stage], (layer, flip(order[stage])))

    cube_copies = [[cube(c, s) for s in range(bits)] for c in range(chunks)]

    halo_copies = []
    for hop in range(halo):
        slot = halo - 1 - hop
        place, source = pl.ds(slot * rows, rows), pl.ds((slot + 1) * rows, rows)
        pairs = (
            (k_ref if hop == 0 else keys.at[:, source], keys.at[:, place]),
            (v_ref if hop == 0 else values.at[:, source], values.at[:, place]),
            (doc_ref if hop == 0 else docs.at[slot + 1], docs.at[slot]),
        )
        halo_copies.append(
            [
                remote(src, dst, halo_send.at[hop, i], halo_recv.at[hop, i], (layer, shifted(1)))
                for i, (src, dst) in enumerate(pairs)
            ]
        )

    for copy in z_copies[0]:
        copy.start()
    for copy in halo_copies[0]:
        copy.start()
    for c in range(1, chunks):
        for copy in z_copies[c]:
            copy.start()

    keys[:, back:] = k_ref[...]
    values[:, back:] = v_ref[...]
    docs[halo] = doc_ref[...]

    def heads(ref, b, start):
        return jnp.concatenate(
            [ref[b, :, start + h * HEAD_SIZE:start + (h + 1) * HEAD_SIZE] for h in range(GROUP)], 0
        )

    def mask():
        qpos = lax.broadcasted_iota(jnp.int32, (rows, rows), 0) + back
        kpos = lax.broadcasted_iota(jnp.int32, (rows, rows), 1)
        for j in range(halo + 1):
            causal = (kpos + j * rows <= qpos) & (kpos + (j + me) * rows >= back)
            for b in range(seqs):
                same = docs[j, b] == docq_ref[b]
                bias[b, :, j * rows:(j + 1) * rows] = jnp.where(causal & same, 0.0, -1e30).astype(F32)

    def forward(g):
        cols = slice(g * HEAD_SIZE, (g + 1) * HEAD_SIZE)

        @pl.loop(0, seqs)
        def _(b):
            s = lax.dot_general(heads(q_ref, b, g * GROUP_WIDTH), keys[b, :, cols], NT, preferred_element_type=F32)
            s = s.reshape(GROUP, rows, window) * scale + bias[b][None]
            e = jnp.exp(s - jnp.max(s, axis=2, keepdims=True))
            p = e / jnp.sum(e, axis=2, keepdims=True)
            probs[g * seqs + b] = p.reshape(GROUP * rows, window).astype(BF16)

    def project(g):
        d = None
        span = slice(g * per_group, (g + 1) * per_group)
        for j in range(depth):
            at = pl.ds(pl.multiple_of(lax.rem(layer + j, depth) * block, block), block)
            w = w_ref[span] if j == 0 else weight[(span,) + (slice(None),) * bits + (j,)]
            term = lax.dot_general(
                grad_ref[:, at], w.reshape(GROUP_WIDTH, block), NT, preferred_element_type=F32
            )
            d = term if d is None else d + term
        dctx[...] = d.astype(BF16).reshape(seqs, rows, GROUP_WIDTH)

    def returned(g, j):
        return remote(
            parts.at[g, j], landed.at[g, j], back_send.at[g, j], back_recv.at[g, j], (layer, shifted(-1))
        )

    back_copies = [[returned(g, j) for j in range(halo)] for g in range(KEY_VALUE_HEADS)]

    def backward(g):
        cols = slice(g * HEAD_SIZE, (g + 1) * HEAD_SIZE)

        @pl.loop(0, seqs)
        def _(b):
            q = heads(q_ref, b, g * GROUP_WIDTH)
            do = heads(dctx, b, 0)
            k = keys[b, :, cols]
            p_low = probs[g * seqs + b]
            dp = lax.dot_general(do, values[b, :, cols], NT, preferred_element_type=F32)
            p = p_low.astype(F32)
            delta = jnp.sum(p * dp, axis=1, keepdims=True)
            ds = (p * (dp - delta)).astype(BF16)
            dq = (jnp.dot(ds, k, preferred_element_type=F32) * scale).astype(BF16)
            for h in range(GROUP):
                start = g * GROUP_WIDTH + h * HEAD_SIZE
                dq_ref[b, :, start:start + HEAD_SIZE] = dq[h * rows:(h + 1) * rows]
            dk = lax.dot_general(ds, q, TN, preferred_element_type=F32) * scale
            dv = lax.dot_general(p_low, do, TN, preferred_element_type=F32)
            for i, term in enumerate((dk, dv)):
                for j in range(halo):
                    parts[g, j, i, b] = term[j * rows:(j + 1) * rows].astype(BF16)
                own[g, i, b] = term[back:]

        back_copies[g][0].start()

    def relay(g):
        for j in range(1, halo):
            back_copies[g][j - 1].wait_recv()
            parts[g, j] = (parts[g, j].astype(F32) + landed[g, j - 1].astype(F32)).astype(BF16)
            back_copies[g][j].start()

    def finish(g):
        cols = slice(g * HEAD_SIZE, (g + 1) * HEAD_SIZE)
        back_copies[g][halo - 1].wait_recv()
        for i, out in enumerate((dk_ref, dv_ref)):
            out[:, :, cols] = (own[g, i] + landed[g, halo - 1, i].astype(F32)).astype(BF16)

    for step in range(chunks + LAG * bits):
        for stage in range(bits, -1, -1):
            c = step - LAG * stage
            if not 0 <= c < chunks:
                continue
            if stage == 0:
                for copy in z_copies[c]:
                    copy.wait_recv()
            else:
                cube_copies[c][stage - 1].wait_recv()
            if stage < bits:
                cube_copies[c][stage].start()
        if step < halo:
            for copy in halo_copies[step]:
                copy.wait_recv()
            if step + 1 < halo:
                for copy in halo_copies[step + 1]:
                    copy.start()
            else:
                mask()
        if 0 <= step - halo - 1 < KEY_VALUE_HEADS:
            forward(step - halo - 1)
        c = step - LAG * bits
        if c >= 0 and c % per_group == per_group - 1:
            group = c // per_group
            project(group)
            if group > 0:
                relay(group - 1)
            backward(group)
            if group > 0:
                finish(group - 1)
    relay(KEY_VALUE_HEADS - 1)
    finish(KEY_VALUE_HEADS - 1)

    for copy in sum(halo_copies, []) + sum(z_copies, []) + sum(cube_copies, []) + sum(back_copies, []):
        copy.wait_send()


def body(grad_out, query_in, rotated_key_input, value_input_columns, out_weight, doc_ids):
    n, depth = lax.axis_size("seq"), lax.axis_size("dp")
    rows, seqs, width = query_in.shape
    features, block = out_weight.shape
    bits = n.bit_length() - 1
    halo = -(-(MAXDOC - 1) // rows)
    window = (halo + 1) * rows
    kv_width = rotated_key_input.shape[2]
    chunks = KEY_VALUE_HEADS * max(1, min(2, features // (KEY_VALUE_HEADS * n * 16)))
    sub = features // (chunks * n)
    cube = (chunks,) + (2,) * bits

    def swap(x):
        return jnp.transpose(x, (1, 0, 2))

    q, grad = swap(query_in), swap(grad_out).reshape(seqs * rows, grad_out.shape[2])
    shapes = (
        jax.ShapeDtypeStruct((seqs, rows, width), BF16),
        jax.ShapeDtypeStruct((seqs, rows, kv_width), BF16),
        jax.ShapeDtypeStruct((seqs, rows, kv_width), BF16),
    )
    dma = pltpu.SemaphoreType.DMA
    dq, dk, dv = pl.pallas_call(
        functools.partial(attention_kernel, n, depth, halo, chunks),
        out_shape=shapes,
        in_specs=[pl.BlockSpec(memory_space=pltpu.VMEM)] * 7,
        out_specs=[pl.BlockSpec(memory_space=pltpu.VMEM)] * 3,
        scratch_shapes=[
            pltpu.VMEM((seqs, rows, window), F32),
            pltpu.VMEM((KEY_VALUE_HEADS * seqs, GROUP * rows, window), BF16),
            pltpu.VMEM((seqs, rows, GROUP_WIDTH), BF16),
            pltpu.VMEM(cube + (depth, sub, block), BF16),
            pltpu.VMEM((seqs, window, kv_width), BF16),
            pltpu.VMEM((seqs, window, kv_width), BF16),
            pltpu.VMEM((halo + 1, seqs, 1, rows), jnp.int32),
            pltpu.VMEM((KEY_VALUE_HEADS, halo, 2, seqs, rows, HEAD_SIZE), BF16),
            pltpu.VMEM((KEY_VALUE_HEADS, halo, 2, seqs, rows, HEAD_SIZE), BF16),
            pltpu.VMEM((KEY_VALUE_HEADS, 2, seqs, rows, HEAD_SIZE), F32),
            dma((chunks, depth - 1)),
            dma((chunks, depth - 1)),
            dma((chunks, bits)),
            dma((chunks, bits)),
            dma((halo, 3)),
            dma((halo, 3)),
            dma((KEY_VALUE_HEADS, halo)),
            dma((KEY_VALUE_HEADS, halo)),
        ],
        compiler_params=pltpu.CompilerParams(
            vmem_limit_bytes=48 << 20, collective_id=0, has_side_effects=True
        ),
    )(
        grad, q, swap(rotated_key_input), swap(value_input_columns),
        out_weight.reshape(cube + (sub, block)), doc_ids[:, :, None], doc_ids[:, None, :],
    )
    return swap(dq), swap(dk), swap(dv)


def solution(mesh):
    in_specs = (
        P("seq", "dp", None),
        P("seq", "dp", None),
        P("seq", "dp", None),
        P("seq", "dp", None),
        P(None, "dp"),
        P("dp", "seq"),
    )
    out_specs = (P("seq", "dp", None), P("seq", "dp", None), P("seq", "dp", None))
    return jax.shard_map(body, mesh=mesh, in_specs=in_specs, out_specs=out_specs, check_vma=False)
```
